32 devices in a mesh: groups: 2 (over y), seq: 4 (over z), head: 4 (over x, core).
Axes of the slice: x: 2, y: 2, z: 4, core: 2. Of those that a mesh axis runs over, the one named last changes fastest.
Arguments:
- cand_feats: bfloat16 [32768, 512], P(('groups', 'seq'), 'head'), parts along dimension 0, may hold values from -6 to 6
- w_query: bfloat16 [512, 512], P(None, 'head'), may hold values from -0.25 to 0.25
- w_gate: bfloat16 [512, 512], replicated, may hold values from -0.25 to 0.25
- w_out: bfloat16 [512, 512], replicated, may hold values from -0.25 to 0.25
- w_up: bfloat16 [512, 1024], replicated, may hold values from -0.25 to 0.25
- w_down: bfloat16 [1024, 512], replicated, may hold values from -0.1875 to 0.1875
- norm_gain: float32 [512], replicated, may hold values from 0.5 to 1.5
- cache_keys: bfloat16 [32, 16384, 512], P('groups', 'seq', 'head'), parts along dimension 0, may hold values from -6 to 6
- cache_values: bfloat16 [32, 16384, 512], P('groups', 'seq', 'head'), parts along dimension 0, may hold values from -6 to 6
- history_items: int32 [32, 16384], P('groups', 'seq'), parts along dimension 0, may hold values from 0 to 63
- buckets: int32 [32, 16384], P('groups', 'seq'), parts along dimension 0, may hold values from 0 to 127
- lengths: int32 [32], P('groups'), parts along dimension 0, may hold values from 1 to 16384
- cand_ids: int32 [32, 1024], P('groups'), parts along dimension 0, may hold values from 0 to 63
- bucket_bias: float32 [128, 8], P(None, 'head'), may hold values from -4 to 4
- repeat_bias: float32 [8], P('head'), may hold values from 0.5 to 3
Outputs:
- scored: bfloat16 [32768, 512], P(('groups', 'seq', 'head')), parts along dimension 0
The draws below stay inside these ranges and needn't reach their ends.
There are 2 independent parts, one for each index of `groups`. The reference program is written for one: setup_inputs(seed, part) draws one part's arguments, and reference() takes and returns one part's arrays. A program takes and returns all parts, laid end to end along the dimension named above; an argument that names none is the same for every part. Nothing has to cross between parts.
Inputs may be any that keep to these rules, and one draw needn't show every extreme that they name: `lengths`: history positions at or past a user's length are ignored.
All inputs are finite; a program needn't handle non-finite values.
Results may differ from the reference program's by a relative error of at most 0.014.
Values may be sent and summed in bfloat16 or wider, within the bound.
A program may use at most 192 MiB of HBM per device.

```python
import math
import jax
import jax.numpy as jnp
from jax import lax

U = 16
C = 1024
L = 16384
H = 8
DH = 64
FF = 1024
NB = 128
ID_RANGE = 64
D = 512
CAND = 16384
N_SEQ = 4


def with_ends(entries, rng, smallest, high):
    spot = [jax.random.randint(jax.random.fold_in(rng, axis), (), 0, length) for axis, length in enumerate(entries.shape)]
    widest = entries.shape.index(max(entries.shape))
    neighbour = spot[:widest] + [(spot[widest] + 1) % entries.shape[widest]] + spot[widest + 1:]
    return entries.at[tuple(spot)].set(smallest).at[tuple(neighbour)].set(high)


def block_levels(rng, shape, cuts, least, high):
    gain = 1.0
    for axis_at, shards_of in cuts:
        steps = jax.random.uniform(jax.random.fold_in(jax.random.fold_in(rng, 6), axis_at), (shards_of,), jnp.float32, least / len(cuts), high / len(cuts))
        gain = gain * jnp.repeat(jnp.exp(steps), shape[axis_at] // shards_of).reshape((-1,) + (1,) * (len(shape) - 1 - axis_at))
    return gain


def normal_values(rng, shape, width, reach, split=(), kind=jnp.bfloat16):
    drawn = jax.random.normal(rng, shape, jnp.float32) * width
    if len(split) > 0:
        drawn = block_levels(rng, shape, split, -0.22, 0.18) * drawn
    return jnp.clip(drawn, min=-reach, max=reach).astype(kind)


def setup_inputs(seed: int = 0, part: int = 0) -> dict:
    key_list = jax.random.split(jax.random.key(seed), 16)
    part_keys = jax.random.split(jax.random.fold_in(key_list[15], part), 16)
    cand_feats = normal_values(part_keys[0], (CAND, D), 1.0, 6.0, ((0, 4), (1, 4)))
    w_query = normal_values(key_list[1], (D, D), D ** -0.5, 0.25, ((1, 4),))
    w_gate = normal_values(key_list[2], (D, D), D ** -0.5, 0.25)
    w_out = normal_values(key_list[3], (D, D), D ** -0.5, 0.25)
    w_up = normal_values(key_list[4], (D, FF), D ** -0.5, 0.25)
    w_down = normal_values(key_list[5], (FF, D), FF ** -0.5, 0.1875)
    norm_gain = jnp.clip(1.0 + 0.1 * jax.random.normal(key_list[6], (D,), jnp.float32), 0.5, 1.5)
    cache_keys = normal_values(part_keys[7], (U, L, D), 1.0, 6.0, ((1, 4), (2, 4)))
    cache_values = normal_values(part_keys[8], (U, L, D), 1.0, 6.0, ((1, 4), (2, 4)))
    history_items = with_ends(jax.random.randint(part_keys[9], (U, L), 0, ID_RANGE), jax.random.fold_in(part_keys[9], 1), 0, ID_RANGE - 1).astype(jnp.int32)
    buckets = with_ends(jax.random.randint(part_keys[10], (U, L), 0, NB), jax.random.fold_in(part_keys[10], 1), 0, NB - 1).astype(jnp.int32)
    lengths = with_ends(jax.random.randint(part_keys[11], (U,), 1, L + 1), jax.random.fold_in(part_keys[11], 1), 1, L).astype(jnp.int32)
    cand_ids = with_ends(jax.random.randint(part_keys[12], (U, C), 0, ID_RANGE), jax.random.fold_in(part_keys[12], 1), 0, ID_RANGE - 1).astype(jnp.int32)
    bucket_bias = normal_values(key_list[13], (NB, H), 1.0, 4.0, ((1, 4),), jnp.float32)
    repeat_bias = jnp.clip(jnp.exp(math.log(3.0) - 1.7917595 * jax.random.uniform(key_list[14], (H,), jnp.float32) ** block_levels(key_list[14], (H,), ((0, 4),), -0.2, 0.2)), 0.5, 3.0)
    return {"cand_feats": cand_feats, "w_query": w_query, "w_gate": w_gate, "w_out": w_out, "w_up": w_up, "w_down": w_down, "norm_gain": norm_gain, "cache_keys": cache_keys, "cache_values": cache_values, "history_items": history_items, "buckets": buckets, "lengths": lengths, "cand_ids": cand_ids, "bucket_bias": bucket_bias, "repeat_bias": repeat_bias}


def silu_value(value):
    return value / (1.0 + jnp.exp(-value))

def attend_block(query_user, key_slab, value_slab, item_slab, bucket_slab, first_pos, user_length, cand_row, bias_table, repeat_gain, shard_span):
    block_size = key_slab.shape[0]
    local_heads = query_user.shape[1]
    group_count = block_size // shard_span
    scores = jnp.einsum('chd,khd->chk', query_user.astype(jnp.float32), key_slab.astype(jnp.float32))
    onehot_table = (bucket_slab[:, None] == jnp.arange(bias_table.shape[0], dtype=jnp.int32)[None, :]).astype(jnp.float32)
    offset = jnp.dot(onehot_table, bias_table, precision=lax.Precision.HIGHEST)
    repeat_hits = (cand_row[:, None] == item_slab[None, :]).astype(jnp.float32)
    scale = 1.0 / math.sqrt(query_user.shape[2])
    scores = scores * scale + offset.T[None, :, :] + repeat_gain[None, :, None] * repeat_hits[:, None, :]
    positions = first_pos + jnp.arange(block_size, dtype=jnp.int32)
    live_mask = (positions < user_length).astype(jnp.float32)
    weights = (silu_value(scores) * live_mask[None, None, :]).astype(jnp.bfloat16)
    weights = weights.reshape(query_user.shape[0], local_heads, group_count, shard_span)
    grouped = value_slab.reshape(group_count, shard_span, local_heads, value_slab.shape[2])
    block_parts = jnp.einsum('chgk,gkhd->gchd', weights.astype(jnp.float32), grouped.astype(jnp.float32))
    rounded = lax.optimization_barrier(block_parts.astype(jnp.bfloat16))
    return lax.optimization_barrier(jnp.sum(rounded.astype(jnp.float32), axis=0))

def reference(cand_feats, w_query, w_gate, w_out, w_up, w_down, norm_gain, cache_keys, cache_values, history_items, buckets, lengths, cand_ids, bucket_bias, repeat_bias):
    shard_span = L // N_SEQ
    group_count = math.gcd(N_SEQ, max(1, 512 // shard_span))
    block_size = shard_span * group_count
    slabs = L // block_size
    queries_all = jnp.dot(cand_feats, w_query, preferred_element_type=jnp.float32).astype(jnp.bfloat16)
    queries_all = queries_all.reshape(U, C, H, DH)
    keyed = cache_keys.reshape(U, slabs, block_size, H, DH)
    valued = cache_values.reshape(U, slabs, block_size, H, DH)
    item_rows = history_items.reshape(U, slabs, block_size)
    bucket_rows = buckets.reshape(U, slabs, block_size)
    starts = jnp.arange(slabs, dtype=jnp.int32) * block_size

    def one_user(inputs):
        query_user, key_user, value_user, item_user, bucket_user, user_length, cand_row = inputs

        def scan_step(running, slab_piece):
            key_slab, value_slab, item_slab, bucket_slab, first_pos = slab_piece
            added = attend_block(query_user, key_slab, value_slab, item_slab, bucket_slab, first_pos, user_length, cand_row, bucket_bias, repeat_bias, shard_span)
            return (running + added, None)
        running, _ = lax.scan(scan_step, jnp.zeros((C, H, DH), jnp.float32), (key_user, value_user, item_user, bucket_user, starts))
        return running
    attended = lax.map(one_user, (queries_all, keyed, valued, item_rows, bucket_rows, lengths, cand_ids))
    attended = attended.reshape(U * C, H * DH)
    center = attended - lax.optimization_barrier(jnp.mean(attended, axis=1, keepdims=True))
    normed = center * lax.rsqrt(lax.optimization_barrier(jnp.mean(center * center, axis=1, keepdims=True)) + 1e-05) * norm_gain[None, :]
    gate_value = silu_value(jnp.dot(cand_feats, w_gate, preferred_element_type=jnp.float32))
    mixed = (normed * gate_value).astype(jnp.bfloat16)
    state_sum = cand_feats.astype(jnp.float32) + jnp.dot(mixed, w_out, preferred_element_type=jnp.float32)
    hidden = silu_value(jnp.dot(state_sum.astype(jnp.bfloat16), w_up, preferred_element_type=jnp.float32)).astype(jnp.bfloat16)
    return (state_sum + jnp.dot(hidden, w_down, preferred_element_type=jnp.float32)).astype(jnp.bfloat16)
```

```python
import functools
import math

import jax
import jax.numpy as jnp
from jax import lax
from jax.experimental import pallas as pl
from jax.experimental.pallas import tpu as pltpu
from jax.sharding import PartitionSpec as P

DH = 64
ITEMS = 64
LANES = 2 * DH
KEYS = 1024
ROWS = 1024


def silu_value(value):
    return value / (1.0 + jnp.exp(-value))


def attend_kernel(
    live_ref,
    gain_ref,
    q_ref,
    same_ref,
    tail_ref,
    key_ref,
    value_ref,
    item_ref,
    bucket_ref,
    table_ref,
    out_ref,
    q_first,
    q_second,
    total,
    *,
    keys,
    rows,
    first_user,
):
    pair = pl.program_id(0)
    user = pl.program_id(1)
    live = live_ref[first_user + user]
    low_lanes = lax.broadcasted_iota(jnp.int32, (1, LANES), 1) < DH
    low_row = low_lanes.astype(jnp.bfloat16)
    high_row = 1 - low_row
    queries = q_ref[...]
    same = same_ref[0]
    q_first[:, :LANES] = queries * low_row + same * high_row
    q_second[:, :LANES] = same * low_row + queries * high_row
    q_first[:, LANES:] = tail_ref[0]
    q_second[:, LANES:] = tail_ref[0]
    total[...] = jnp.zeros_like(total)
    table = table_ref[pair]

    def step(index, carry):
        start = pl.multiple_of(index * keys, keys)
        window = pl.ds(start, keys)
        keyed = key_ref[0, window, :].T
        items = item_ref[0, :, window]
        hits = lax.broadcasted_iota(jnp.int32, (ITEMS, keys), 0) == items
        bucket_hits = (
            lax.broadcasted_iota(jnp.int32, (table.shape[1], keys), 0) == bucket_ref[0, :, window]
        )
        bias = jnp.dot(
            table,
            bucket_hits.astype(jnp.float32).astype(jnp.bfloat16),
            preferred_element_type=jnp.float32,
        ).astype(jnp.bfloat16)

        def gains(which):
            return jnp.where(hits, gain_ref[pair, which], 0.0).astype(jnp.bfloat16)

        depth_first = jnp.concatenate([keyed[:DH], gains(0), gains(1), bias[:DH]], axis=0)
        depth_second = jnp.concatenate([gains(2), keyed[DH:], gains(3), bias[DH:]], axis=0)
        place = start + lax.broadcasted_iota(jnp.int32, (keys, LANES), 0)
        lane = lax.broadcasted_iota(jnp.int32, (keys, LANES), 1)
        values = value_ref[0, window, :].astype(jnp.float32)
        alive = place < live
        values_first = jnp.where(alive & (lane < DH), values, 0.0).astype(jnp.bfloat16)
        values_second = jnp.where(alive & (lane >= DH), values, 0.0).astype(jnp.bfloat16)
        for base in range(0, total.shape[0], rows):
            span = slice(base, base + rows)
            half = jnp.dot(q_first[span, :], depth_first, preferred_element_type=jnp.float32)
            act_first = (half + half * jnp.tanh(half)).astype(jnp.bfloat16)
            half = jnp.dot(q_second[span, :], depth_second, preferred_element_type=jnp.float32)
            act_second = (half + half * jnp.tanh(half)).astype(jnp.bfloat16)
            total[span, :] += jnp.dot(
                act_first, values_first, preferred_element_type=jnp.float32
            ) + jnp.dot(act_second, values_second, preferred_element_type=jnp.float32)
        return carry

    count = key_ref.shape[1] // keys
    used = jnp.clip((live + keys - 1) // keys, 0, count)
    lax.fori_loop(0, used, step, 0)
    out_ref[...] = total[...].astype(out_ref.dtype)


def attend(queries, packed, first_user, user_count):
    live, gains, same, tail, keys_all, values_all, items, buckets, table = packed
    per_user = same.shape[1]
    width = queries.shape[1]
    pairs = width // LANES
    span = keys_all.shape[1]
    keys = math.gcd(span, KEYS)
    rows = math.gcd(per_user, ROWS)
    of_user = lambda p, u, *_: (first_user + u, 0, 0)
    of_pair = lambda p, u, *_: (first_user + u, 0, p)
    scores = user_count * per_user * span * 2 * pairs
    return pl.pallas_call(
        functools.partial(attend_kernel, keys=keys, rows=rows, first_user=first_user),
        out_shape=jax.ShapeDtypeStruct(queries.shape, jnp.bfloat16),
        grid_spec=pltpu.PrefetchScalarGridSpec(
            num_scalar_prefetch=2,
            grid=(pairs, user_count),
            in_specs=[
                pl.BlockSpec((per_user, LANES), lambda p, u, *_: (u, p)),
                pl.BlockSpec((1, per_user, LANES), of_user),
                pl.BlockSpec((1, per_user, LANES), of_user),
                pl.BlockSpec((1, span, LANES), of_pair),
                pl.BlockSpec((1, span, LANES), of_pair),
                pl.BlockSpec((1, 1, span), of_user),
                pl.BlockSpec((1, 1, span), of_user),
                pl.BlockSpec(table.shape, lambda p, u, *_: (0, 0, 0)),
            ],
            out_specs=pl.BlockSpec((per_user, LANES), lambda p, u, *_: (u, p)),
            scratch_shapes=[
                pltpu.VMEM((per_user, 2 * LANES), jnp.bfloat16),
                pltpu.VMEM((per_user, 2 * LANES), jnp.bfloat16),
                pltpu.VMEM((per_user, LANES), jnp.float32),
            ],
        ),
        compiler_params=pltpu.CompilerParams(
            dimension_semantics=("arbitrary", "arbitrary"), vmem_limit_bytes=56 << 20
        ),
        cost_estimate=pl.CostEstimate(
            flops=scores * 512,
            bytes_accessed=4 * user_count * (span + per_user) * width,
            transcendentals=scores,
        ),
    )(live, gains, queries, same, tail, keys_all, values_all, items, buckets, table)


def split_parts(value, count):
    parts = []
    for _ in range(count):
        part = lax.reduce_precision(value, 8, 7)
        parts.append(part)
        value = value - part
    return parts


def pack_tables(keys_all, values_all, items, buckets, lengths, cand_ids, bias_table, gain, first_pos):
    width = keys_all.shape[2]
    pad = -width % LANES
    heads = (width + pad) // DH
    pairs = heads // 2
    if pad:
        keys_all = jnp.pad(keys_all, ((0, 0), (0, 0), (0, pad)))
        values_all = jnp.pad(values_all, ((0, 0), (0, 0), (0, pad)))
        bias_table = jnp.pad(bias_table, ((0, 0), (0, heads - bias_table.shape[1])))
        gain = jnp.pad(gain, (0, heads - gain.shape[0]))
    live = lengths - first_pos
    gain_high, gain_low = split_parts(gain * 0.5, 2)
    gains = jnp.stack([gain_high, gain_low], axis=1).reshape(pairs, 4)
    parts = jnp.stack(split_parts(bias_table * 0.5, 3), axis=0)
    table = jnp.pad(parts.transpose(2, 0, 1), ((0, 0), (0, DH - 3), (0, 0)))
    table = table.reshape(pairs, LANES, bias_table.shape[0]).astype(jnp.bfloat16)
    lane = jnp.arange(LANES, dtype=jnp.int32)[None, None, :]
    hits = cand_ids[:, :, None] == lane % ITEMS
    same = hits.astype(jnp.bfloat16)
    tail = ((hits & (lane < DH)) | ((lane >= DH) & (lane < DH + 3))).astype(jnp.bfloat16)
    return (
        live,
        gains,
        same,
        tail,
        keys_all,
        values_all,
        items[:, None, :],
        buckets[:, None, :],
        table,
    )


def finish(pieces, own_rows, w_gate, w_out, w_up, w_down, norm_gain):
    center = pieces - jnp.mean(pieces, axis=1, keepdims=True)
    normed = (
        center
        * lax.rsqrt(jnp.mean(center * center, axis=1, keepdims=True) + 1e-05)
        * norm_gain[None, :]
    )
    gate_value = silu_value(jnp.dot(own_rows, w_gate, preferred_element_type=jnp.float32))
    mixed = (normed * gate_value).astype(jnp.bfloat16)
    state_sum = own_rows.astype(jnp.float32) + jnp.dot(
        mixed, w_out, preferred_element_type=jnp.float32
    )
    hidden = silu_value(
        jnp.dot(state_sum.astype(jnp.bfloat16), w_up, preferred_element_type=jnp.float32)
    ).astype(jnp.bfloat16)
    return (state_sum + jnp.dot(hidden, w_down, preferred_element_type=jnp.float32)).astype(
        jnp.bfloat16
    )


def local(
    cand_feats,
    w_query,
    w_gate,
    w_out,
    w_up,
    w_down,
    norm_gain,
    cache_keys,
    cache_values,
    history_items,
    buckets,
    lengths,
    cand_ids,
    bucket_bias,
    repeat_bias,
):
    user_count = lengths.shape[0]
    span = cache_keys.shape[1]
    width = cache_keys.shape[2]
    pad = -width % LANES
    packed = pack_tables(
        cache_keys,
        cache_values,
        history_items,
        buckets,
        lengths,
        cand_ids,
        bucket_bias,
        repeat_bias,
        lax.axis_index("seq") * span,
    )
    features = lax.all_gather(cand_feats, "head", axis=1, tiled=True)
    queries_own = jnp.dot(features, w_query, preferred_element_type=jnp.float32).astype(
        jnp.bfloat16
    ) * (0.5 / math.sqrt(DH))
    gathered = lax.all_gather(queries_own, "seq", axis=0, tiled=True)
    if pad:
        gathered = jnp.pad(gathered, ((0, 0), (0, pad)))
    partial_rows = attend(gathered, packed, 0, user_count)[:, :width]
    own_sum = lax.psum_scatter(partial_rows, "seq", scatter_dimension=0, tiled=True)
    pieces = lax.all_to_all(own_sum, "head", split_axis=0, concat_axis=1, tiled=True).astype(
        jnp.float32
    )
    row_count = pieces.shape[0]
    own_rows = lax.dynamic_slice_in_dim(features, lax.axis_index("head") * row_count, row_count, 0)
    return finish(pieces, own_rows, w_gate, w_out, w_up, w_down, norm_gain)


def solution(mesh):
    in_specs = (
        P(("groups", "seq"), "head"),
        P(None, "head"),
        P(),
        P(),
        P(),
        P(),
        P(),
        P("groups", "seq", "head"),
        P("groups", "seq", "head"),
        P("groups", "seq"),
        P("groups", "seq"),
        P("groups"),
        P("groups", None),
        P(None, "head"),
        P("head"),
    )
    out_specs = P(("groups", "seq", "head"), None)
    return jax.shard_map(local, mesh=mesh, in_specs=in_specs, out_specs=out_specs, check_vma=False)
```

```python
import functools
import math

import jax
import jax.numpy as jnp
from jax import lax
from jax.experimental import pallas as pl
from jax.experimental.pallas import tpu as pltpu
from jax.sharding import PartitionSpec as P

DH = 64
ITEMS = 64
LANES = 2 * DH
KEYS = 1024
ROWS = 1024


def silu_value(value):
    return value / (1.0 + jnp.exp(-value))


def attend_kernel(
    live_ref,
    gain_ref,
    q_ref,
    same_ref,
    tail_ref,
    key_ref,
    value_ref,
    item_ref,
    bucket_ref,
    table_ref,
    out_ref,
    q_first,
    q_second,
    total,
    *,
    keys,
    rows,
    offset,
    stride,
):
    pair = pl.program_id(0)
    user = pl.program_id(1)
    live = live_ref[user * stride + offset]
    low_lanes = lax.broadcasted_iota(jnp.int32, (1, LANES), 1) < DH
    low_row = low_lanes.astype(jnp.bfloat16)
    high_row = 1 - low_row
    queries = q_ref[...]
    same = same_ref[0]
    q_first[:, :LANES] = queries * low_row + same * high_row
    q_second[:, :LANES] = same * low_row + queries * high_row
    q_first[:, LANES:] = tail_ref[0]
    q_second[:, LANES:] = tail_ref[0]
    total[...] = jnp.zeros_like(total)
    table = table_ref[pair]

    def step(index, carry):
        start = pl.multiple_of(index * keys, keys)
        window = pl.ds(start, keys)
        keyed = key_ref[0, window, :].T
        items = item_ref[0, :, window]
        hits = lax.broadcasted_iota(jnp.int32, (ITEMS, keys), 0) == items
        bucket_hits = (
            lax.broadcasted_iota(jnp.int32, (table.shape[1], keys), 0) == bucket_ref[0, :, window]
        )
        bias = jnp.dot(
            table,
            bucket_hits.astype(jnp.float32).astype(jnp.bfloat16),
            preferred_element_type=jnp.float32,
        ).astype(jnp.bfloat16)

        def gains(which):
            return jnp.where(hits, gain_ref[pair, which], 0.0).astype(jnp.bfloat16)

        depth_first = jnp.concatenate([keyed[:DH], gains(0), gains(1), bias[:DH]], axis=0)
        depth_second = jnp.concatenate([gains(2), keyed[DH:], gains(3), bias[DH:]], axis=0)
        place = start + lax.broadcasted_iota(jnp.int32, (keys, LANES), 0)
        lane = lax.broadcasted_iota(jnp.int32, (keys, LANES), 1)
        values = value_ref[0, window, :].astype(jnp.float32)
        alive = place < live
        values_first = jnp.where(alive & (lane < DH), values, 0.0).astype(jnp.bfloat16)
        values_second = jnp.where(alive & (lane >= DH), values, 0.0).astype(jnp.bfloat16)
        for base in range(0, total.shape[0], rows):
            span = slice(base, base + rows)
            half = jnp.dot(q_first[span, :], depth_first, preferred_element_type=jnp.float32)
            act_first = (half + half * jnp.tanh(half)).astype(jnp.bfloat16)
            half = jnp.dot(q_second[span, :], depth_second, preferred_element_type=jnp.float32)
            act_second = (half + half * jnp.tanh(half)).astype(jnp.bfloat16)
            total[span, :] += jnp.dot(
                act_first, values_first, preferred_element_type=jnp.float32
            ) + jnp.dot(act_second, values_second, preferred_element_type=jnp.float32)
        return carry

    count = key_ref.shape[1] // keys
    used = jnp.clip((live + keys - 1) // keys, 0, count)
    lax.fori_loop(0, used, step, 0)
    out_ref[...] = total[...].astype(out_ref.dtype)


def attend(queries, packed, offset, stride, base=0, user_count=None):
    live, gains, same, tail, keys_all, values_all, items, buckets, table = packed
    per_user = same.shape[1]
    user_count = user_count or queries.shape[0] // per_user
    offset = offset + base * stride
    width = queries.shape[1]
    pairs = width // LANES
    span = keys_all.shape[1]
    keys = math.gcd(span, KEYS)
    rows = math.gcd(per_user, ROWS)
    of_user = lambda p, u, *_: (u * stride + offset, 0, 0)
    of_pair = lambda p, u, *_: (u * stride + offset, 0, p)
    scores = user_count * per_user * span * 2 * pairs
    return pl.pallas_call(
        functools.partial(attend_kernel, keys=keys, rows=rows, offset=offset, stride=stride),
        out_shape=jax.ShapeDtypeStruct((user_count * per_user, width), jnp.bfloat16),
        grid_spec=pltpu.PrefetchScalarGridSpec(
            num_scalar_prefetch=2,
            grid=(pairs, user_count),
            in_specs=[
                pl.BlockSpec((per_user, LANES), lambda p, u, *_: (u + base, p)),
                pl.BlockSpec((1, per_user, LANES), of_user),
                pl.BlockSpec((1, per_user, LANES), of_user),
                pl.BlockSpec((1, span, LANES), of_pair),
                pl.BlockSpec((1, span, LANES), of_pair),
                pl.BlockSpec((1, 1, span), of_user),
                pl.BlockSpec((1, 1, span), of_user),
                pl.BlockSpec(table.shape, lambda p, u, *_: (0, 0, 0)),
            ],
            out_specs=pl.BlockSpec((per_user, LANES), lambda p, u, *_: (u, p)),
            scratch_shapes=[
                pltpu.VMEM((per_user, 2 * LANES), jnp.bfloat16),
                pltpu.VMEM((per_user, 2 * LANES), jnp.bfloat16),
                pltpu.VMEM((per_user, LANES), jnp.float32),
            ],
        ),
        compiler_params=pltpu.CompilerParams(
            dimension_semantics=("arbitrary", "arbitrary"), vmem_limit_bytes=56 << 20
        ),
        cost_estimate=pl.CostEstimate(
            flops=scores * 512,
            bytes_accessed=4 * user_count * (span + per_user) * width,
            transcendentals=scores,
        ),
    )(live, gains, queries, same, tail, keys_all, values_all, items, buckets, table)


def split_parts(value, count):
    parts = []
    for _ in range(count):
        part = lax.reduce_precision(value, 8, 7)
        parts.append(part)
        value = value - part
    return parts


def pack_tables(keys_all, values_all, items, buckets, lengths, cand_ids, bias_table, gain, first_pos):
    width = keys_all.shape[2]
    pad = -width % LANES
    heads = (width + pad) // DH
    pairs = heads // 2
    if pad:
        keys_all = jnp.pad(keys_all, ((0, 0), (0, 0), (0, pad)))
        values_all = jnp.pad(values_all, ((0, 0), (0, 0), (0, pad)))
        bias_table = jnp.pad(bias_table, ((0, 0), (0, heads - bias_table.shape[1])))
        gain = jnp.pad(gain, (0, heads - gain.shape[0]))
    live = lengths - first_pos
    gain_high, gain_low = split_parts(gain * 0.5, 2)
    gains = jnp.stack([gain_high, gain_low], axis=1).reshape(pairs, 4)
    parts = jnp.stack(split_parts(bias_table * 0.5, 3), axis=0)
    table = jnp.pad(parts.transpose(2, 0, 1), ((0, 0), (0, DH - 3), (0, 0)))
    table = table.reshape(pairs, LANES, bias_table.shape[0]).astype(jnp.bfloat16)
    lane = jnp.arange(LANES, dtype=jnp.int32)[None, None, :]
    hits = cand_ids[:, :, None] == lane % ITEMS
    same = hits.astype(jnp.bfloat16)
    tail = ((hits & (lane < DH)) | ((lane >= DH) & (lane < DH + 3))).astype(jnp.bfloat16)
    return (
        live,
        gains,
        same,
        tail,
        keys_all,
        values_all,
        items[:, None, :],
        buckets[:, None, :],
        table,
    )


def finish(pieces, own_rows, w_gate, w_out, w_up, w_down, norm_gain):
    center = pieces - jnp.mean(pieces, axis=1, keepdims=True)
    normed = (
        center
        * lax.rsqrt(jnp.mean(center * center, axis=1, keepdims=True) + 1e-05)
        * norm_gain[None, :]
    )
    gate_value = silu_value(jnp.dot(own_rows, w_gate, preferred_element_type=jnp.float32))
    mixed = (normed * gate_value).astype(jnp.bfloat16)
    state_sum = own_rows.astype(jnp.float32) + jnp.dot(
        mixed, w_out, preferred_element_type=jnp.float32
    )
    hidden = silu_value(
        jnp.dot(state_sum.astype(jnp.bfloat16), w_up, preferred_element_type=jnp.float32)
    ).astype(jnp.bfloat16)
    return (state_sum + jnp.dot(hidden, w_down, preferred_element_type=jnp.float32)).astype(
        jnp.bfloat16
    )


def local(
    cand_feats,
    w_query,
    w_gate,
    w_out,
    w_up,
    w_down,
    norm_gain,
    cache_keys,
    cache_values,
    history_items,
    buckets,
    lengths,
    cand_ids,
    bucket_bias,
    repeat_bias,
):
    span = cache_keys.shape[1]
    width = cache_keys.shape[2]
    pad = -width % LANES
    packed = pack_tables(
        cache_keys,
        cache_values,
        history_items,
        buckets,
        lengths,
        cand_ids,
        bucket_bias,
        repeat_bias,
        lax.axis_index("seq") * span,
    )
    heads = lax.axis_size("head")
    per_user = cand_ids.shape[1]
    own_users = cand_feats.shape[0] // per_user

    def project(features):
        product = jnp.dot(features, w_query, preferred_element_type=jnp.float32)
        return product.astype(jnp.bfloat16) * (0.5 / math.sqrt(DH))

    if cand_feats.shape[0] % per_user or own_users != heads:
        features = lax.all_gather(cand_feats, "head", axis=1, tiled=True)
        gathered = lax.all_gather(project(features), "seq", axis=0, tiled=True)
        if pad:
            gathered = jnp.pad(gathered, ((0, 0), (0, pad)))
        partial_rows = attend(gathered, packed, 0, 1)[:, :width]
        own_sum = lax.psum_scatter(partial_rows, "seq", scatter_dimension=0, tiled=True)
        row_count = cand_feats.shape[0] // heads
        own_rows = lax.dynamic_slice_in_dim(
            features, lax.axis_index("head") * row_count, row_count, 0
        )
    else:
        shards = lax.axis_size("seq")
        after = lax.optimization_barrier
        rows = [cand_feats[user * per_user : (user + 1) * per_user] for user in range(own_users)]

        def over_head(user):
            return lax.all_gather(rows[user], "head", axis=1, tiled=True)

        def over_seq(queries):
            whole = lax.all_gather(queries, "seq", axis=0, tiled=True)
            return jnp.pad(whole, ((0, 0), (0, pad))) if pad else whole

        def summed(part):
            return lax.psum_scatter(part[:, :width], "seq", scatter_dimension=0, tiled=True)

        features = [over_head(0)]
        arrived = [over_seq(project(features[0]))]
        for user in range(1, min(3, own_users)):
            rows[user], arrived[0] = after((rows[user], arrived[0]))
            features.append(over_head(user))
        early = max(1, shards // 2)
        part = attend(arrived[0], packed, 0, own_users, 0, early)
        sums = []
        for user in range(own_users):
            if user + 1 < own_users:
                features[user + 1], part = after((features[user + 1], part))
                queries = project(features[user + 1])
                queries, arrived[user] = after((queries, arrived[user]))
                arrived.append(over_seq(queries))
            if user == 0:
                if shards > early:
                    rest = attend(arrived[0], packed, 0, own_users, early, shards - early)
                    part = jnp.concatenate([part, rest], axis=0)
            else:
                arrived[user], part = after((arrived[user], part))
                sums.append(summed(part))
                part = attend(arrived[user], packed, user, own_users)
            if user + 3 < own_users:
                rows[user + 3], part = after((rows[user + 3], part))
                features.append(over_head(user + 3))
        sums.append(summed(part))
        own_rows = features[0]
        for user in range(1, own_users):
            own_rows = jnp.where(lax.axis_index("head") == user, features[user], own_rows)
        own_sum = jnp.concatenate(sums, axis=0)
    pieces = lax.all_to_all(own_sum, "head", split_axis=0, concat_axis=1, tiled=True).astype(
        jnp.float32
    )
    return finish(pieces, own_rows, w_gate, w_out, w_up, w_down, norm_gain)


def solution(mesh):
    in_specs = (
        P(("groups", "seq"), "head"),
        P(None, "head"),
        P(),
        P(),
        P(),
        P(),
        P(),
        P("groups", "seq", "head"),
        P("groups", "seq", "head"),
        P("groups", "seq"),
        P("groups", "seq"),
        P("groups"),
        P("groups", None),
        P(None, "head"),
        P("head"),
    )
    out_specs = P(("groups", "seq", "head"), None)
    return jax.shard_map(local, mesh=mesh, in_specs=in_specs, out_specs=out_specs, check_vma=False)
```
